768 devices in a mesh: energy: 96 (over y_hi, x, z), kpoint: 2 (over core), tile: 4 (over y_lo).
Axes of the slice: x: 4, y: 8 (y_hi: 2, y_lo: 4; y = y_hi * 4 + y_lo), z: 12, core: 2. Of those that a mesh axis runs over, the one named last changes fastest.
Arguments:
- g_zero: bfloat16 [96, 2, 2, 6, 4, 128, 128], P('energy', 'kpoint', None, None, None, 'tile'), may hold values from -6 to 6
- sigma_prev: bfloat16 [96, 2, 2, 6, 128, 128], P('energy', 'kpoint'), may hold values from -0.0234375 to 0.0234375
- grad_h: bfloat16 [6, 128, 128], replicated, may hold values from -0.5 to 0.5
- cols: int32 [6, 4], replicated, may hold values from 0 to 5, as said below
- shifts: int32 [4], replicated, may hold values from 1 to 6, as said below
- pairs: int32 [2, 4], replicated, may hold values from 0 to 1, as said below
- couple: float32 [2, 4], replicated, may hold values from 0.2 to 1
Outputs:
- g_new: bfloat16 [96, 2, 2, 6, 4, 128, 128], P('energy', 'kpoint', None, None, None, 'tile')
- sigma_new: bfloat16 [96, 2, 2, 6, 128, 128], P('energy', 'kpoint', None, None, 'tile')
The draws below stay inside these ranges and needn't reach their ends.
Inputs may be any that keep to these rules, and one draw needn't show every extreme that they name: `cols`: row i names 4 different column blocks, and its first slot names i itself. `shifts`: some channel has exactly 6. `pairs`: some channel takes each target momentum from the other momentum.
All inputs are finite; a program needn't handle non-finite values.
Results may differ from the reference program's by a relative error of at most 0.0069.
Values may be sent and summed in bfloat16 or wider, within the bound.
No kernel may reach another device: no remote copies, remote signals or barrier semaphores. Data moves between devices by JAX's collectives and lax.ppermute only.
A program may use at most 32 MiB of HBM per device.

```python
import math
import jax
import jax.numpy as jnp
from jax import lax

BS = 128
NB = 6
SLOTS = 4
NQ = 4
WMAX = 6
ENERGIES = 96
MOMENTA = 2


def draw_cols(key, part):
    scores = jax.random.randint(key, (NB, NB), 0, 1 << 20)
    scores = scores * NB + jnp.arange(NB)[None, :]
    diagonal_hit = jnp.arange(NB)[:, None] == jnp.arange(NB)[None, :]
    scores = jnp.where(diagonal_hit, (1 << 20) * NB + NB, scores)
    return lax.top_k(scores, SLOTS)[1].astype(jnp.int32)


def draw_shifts(key, part):
    values = jax.random.randint(key, (NQ,), 1, WMAX + 1)
    chosen_slot = jax.random.randint(jax.random.fold_in(key, 7), (), 0, NQ)
    return jnp.where(jnp.arange(NQ) == chosen_slot, WMAX, values).astype(jnp.int32)


def draw_pairs(key, part):
    offsets = jax.random.randint(key, (NQ,), 0, MOMENTA)
    chosen_slot = jax.random.randint(jax.random.fold_in(key, 3), (), 0, NQ)
    offsets = jnp.where(jnp.arange(NQ) == chosen_slot, 1, offsets)
    target = jnp.arange(MOMENTA)[:, None]
    return ((target + offsets[None, :]) % MOMENTA).astype(jnp.int32)


def shard_levels(own_key, dims, cuts, low, largest):
    level, own = 1.0, jax.random.fold_in(own_key, 6)
    for axis_at, parts in cuts:
        heights = jnp.exp(jax.random.uniform(jax.random.fold_in(own, axis_at), (parts,), jnp.float32, low / len(cuts), largest / len(cuts)))
        level = level * jnp.repeat(heights, dims[axis_at] // parts).reshape([-1 if axis == axis_at else 1 for axis in range(len(dims))])
    return level


def bell_draw(rng, dims, width, bound, cuts=(), kind=jnp.bfloat16):
    drawn = width * jax.random.normal(rng, dims, jnp.float32)
    if cuts:
        drawn = drawn * shard_levels(rng, dims, cuts, -0.22, 0.18)
    return jnp.clip(drawn, -bound, bound).astype(kind)


def setup_inputs(seed: int = 0) -> dict:
    arg_keys = jax.random.split(jax.random.key(seed), 8)
    g_zero = bell_draw(arg_keys[0], (ENERGIES, MOMENTA, 2, NB, SLOTS, BS, BS), 1.0, 6.0, ((0, 96), (1, 2), (5, 4)))
    sigma_prev = bell_draw(arg_keys[1], (ENERGIES, MOMENTA, 2, NB, BS, BS), 0.004, 0.0234375, ((0, 96), (1, 2)))
    grad_h = bell_draw(arg_keys[2], (NB, BS, BS), BS ** -0.5, 0.5)
    cols = draw_cols(jax.random.fold_in(arg_keys[7], 71), 0)
    shifts = draw_shifts(jax.random.fold_in(arg_keys[7], 71), 0)
    pairs = draw_pairs(jax.random.fold_in(arg_keys[7], 71), 0)
    couple = jnp.clip(jnp.exp(jax.random.uniform(arg_keys[6], (2, NQ), jnp.float32, math.log(0.2), math.log(1.0))), 0.2, 1.0)
    return dict(g_zero=g_zero, sigma_prev=sigma_prev, grad_h=grad_h, cols=cols, shifts=shifts, pairs=pairs, couple=couple)


def coupling_table(shifts, pairs, couple, energies, momenta):
    row_energy = jnp.arange(energies)[:, None, None]
    col_energy = jnp.arange(energies)[None, :, None]
    upper_hit = (col_energy == row_energy + shifts[None, None, :]).astype(jnp.float32)
    lower_hit = (col_energy == row_energy - shifts[None, None, :]).astype(jnp.float32)
    energy_part = upper_hit * couple[0][None, None, :] + lower_hit * couple[1][None, None, :]
    source = (pairs[:, None, :] == jnp.arange(momenta)[None, :, None]).astype(jnp.float32)
    return jnp.einsum('efq,kpq->kpef', energy_part, source, precision=lax.Precision.HIGHEST)


def selection(cols):
    block_ids = jnp.arange(cols.shape[0])
    row_names = cols[:, :, None] == block_ids[None, None, :]
    col_hit = cols[None, None, :, :] == cols[:, :, None, None]
    return row_names[:, :, None, :, None] & col_hit[:, None, :, :, :]


def complex_product(formula, left_op, right_op):
    real_part = jnp.einsum(formula, left_op[0], right_op[0]) - jnp.einsum(formula, left_op[1], right_op[1])
    imag_part = jnp.einsum(formula, left_op[0], right_op[1]) + jnp.einsum(formula, left_op[1], right_op[0])
    return jnp.stack([real_part, imag_part])


def dyson_one(g_block, sigma_block, grad_h, cols):
    green = g_block.astype(jnp.float32)
    sigma_cols = sigma_block.astype(jnp.float32)[:, cols]
    a_full = lax.optimization_barrier(complex_product('itab,itbc->itac', green, sigma_cols).astype(jnp.bfloat16)).astype(jnp.float32)
    pick_table = selection(cols).astype(jnp.float32)
    slot_terms = []
    for slot_id in range(cols.shape[1]):
        chosen = jnp.einsum('itmu,rmubc->ritbc', pick_table[:, :, slot_id], green)
        slot_terms.append(complex_product('itab,itbc->iac', a_full, chosen))
    g_new = (green + jnp.stack(slot_terms, axis=2)).astype(jnp.bfloat16)
    diagonal = g_new[:, :, 0].astype(jnp.float32)
    grad_f = grad_h.astype(jnp.float32)
    g_times_m = jnp.stack([jnp.einsum('nab,ncb->nac', diagonal[part_id], grad_f) for part_id in range(2)])
    g_times_m = lax.optimization_barrier(g_times_m.astype(jnp.bfloat16)).astype(jnp.float32)
    sandwiched = jnp.stack([jnp.einsum('nab,nbc->nac', grad_f, g_times_m[part_id]) for part_id in range(2)])
    return g_new, sandwiched.astype(jnp.bfloat16)


def reference(g_zero, sigma_prev, grad_h, cols, shifts, pairs, couple):
    energies, momenta = g_zero.shape[0], g_zero.shape[1]
    flat_g = g_zero.reshape((energies * momenta,) + g_zero.shape[2:])
    flat_s = sigma_prev.reshape((energies * momenta,) + sigma_prev.shape[2:])

    def one_case(inputs):
        return dyson_one(inputs[0], inputs[1], grad_h, cols)

    g_new, sandwiched = lax.map(one_case, (flat_g, flat_s))
    g_new = g_new.reshape(g_zero.shape)
    sandwiched = sandwiched.reshape(energies, momenta, -1).astype(jnp.float32)
    table_w = coupling_table(shifts, pairs, couple, energies, momenta)
    sigma_new = jnp.einsum('kpef,fpx->ekx', table_w, sandwiched, precision=lax.Precision.HIGHEST)
    return g_new, sigma_new.reshape(sigma_prev.shape).astype(jnp.bfloat16)
```

```python
import jax
import jax.numpy as jnp
from jax import lax
from jax.experimental import pallas as pl
from jax.experimental.pallas import tpu as pltpu
from jax.sharding import Mesh, PartitionSpec as P


BS = 128
NB = 6
SLOTS = 4
NQ = 4
WMAX = 6
TILES = 4
ROWS = BS // TILES
Z = 12
LINES = 8
CHUNK = 16


def along_tile(block, step, first, last):
    return lax.ppermute(block, "tile", [(t, t + step) for t in range(first, last + 1)])


def along_lines(block, step):
    route = [(a, a + step) for a in range(LINES) if 0 <= a + step < LINES]
    return lax.ppermute(block, ("yh", "x"), route)


def dot(left, right):
    return jnp.dot(left, right, preferred_element_type=jnp.float32)


def products_kernel(tile_ref, cols_ref, *refs):
    (own_r, own_i, r1r, r1i, l1r, l1i, r2r, r2i, l2r, l2i, r3r, r3i, l3r, l3i) = refs[:14]
    sigma_ref, grad_ref, g_new_ref, sand_ref, dense, prod, weights, sums = refs[14:]
    tile = tile_ref[0]
    from_left = {1: (r1r, r1i), 2: (r2r, r2i), 3: (r3r, r3i)}
    from_right = {1: (l1r, l1i), 2: (l2r, l2i), 3: (l3r, l3i)}

    for i in range(NB):
        for c in range(NB):
            if i == c:
                continue
            present = cols_ref[i, 1] == c
            for s in range(2, SLOTS):
                present = jnp.logical_or(present, cols_ref[i, s] == c)

            @pl.when(jnp.logical_not(present))
            def _(i=i, c=c):
                dense[c, i] = jnp.zeros((2 * BS, 2 * BS), jnp.bfloat16)

    for me in range(TILES):

        @pl.when(tile == me)
        def _(me=me):
            def place(b, carry):
                i = b // SLOTS
                s = b % SLOTS
                c = cols_ref[i, s]
                for p in range(TILES):
                    if p == me:
                        re_ref, im_ref = own_r, own_i
                    elif p < me:
                        re_ref, im_ref = from_left[me - p]
                    else:
                        re_ref, im_ref = from_right[p - me]
                    re = re_ref[i, s]
                    im = im_ref[i, s]
                    top = pl.ds(p * ROWS, ROWS)
                    low = pl.ds(BS + p * ROWS, ROWS)
                    dense[c, i, top, :BS] = re
                    dense[c, i, top, BS:] = im
                    dense[c, i, low, :BS] = -im
                    dense[c, i, low, BS:] = re
                return carry

            lax.fori_loop(0, NB * SLOTS, place, 0)

    for m in range(NB):
        re = sigma_ref[0, m]
        im = sigma_ref[1, m]
        weights[m, :BS, :BS] = re
        weights[m, :BS, BS:] = im
        weights[m, BS:, :BS] = -im
        weights[m, BS:, BS:] = re

    for m in range(NB):
        left = dense[m, :, :BS, :].reshape(NB * BS, 2 * BS)
        a = dot(left, weights[m]).astype(jnp.bfloat16)
        prod[:, :, m * 2 * BS : (m + 1) * 2 * BS] = a.reshape(NB, BS, 2 * BS)

    mine = pl.ds(pl.multiple_of(tile * ROWS, ROWS), ROWS)
    for c in range(NB):
        column = dense[c].reshape(NB * 2 * BS, 2 * BS)
        diag = dot(prod[c], column) + dense[c, c, :BS, :].astype(jnp.float32)
        diag = diag.astype(jnp.bfloat16)
        both = jnp.concatenate([diag[:, :BS], diag[:, BS:]], axis=0)
        g_m = lax.dot_general(
            both, grad_ref[c], (((1,), (1,)), ((), ())), preferred_element_type=jnp.float32
        ).astype(jnp.bfloat16)
        pair = jnp.concatenate([g_m[:BS], g_m[BS:]], axis=1)
        sand = dot(grad_ref[c, mine, :], pair).astype(jnp.bfloat16)
        sand_ref[0, c] = sand[:, :BS]
        sand_ref[1, c] = sand[:, BS:]

    mine_rows = prod[:, mine, :].reshape(NB * ROWS, NB * 2 * BS)
    for c in range(NB):
        sums[c] = dot(mine_rows, dense[c].reshape(NB * 2 * BS, 2 * BS))

    def finish(b, carry):
        i = b // SLOTS
        s = b % SLOTS
        c = cols_ref[i, s]
        value = sums[c, pl.ds(pl.multiple_of(i * ROWS, ROWS), ROWS), :]
        g_new_ref[0, i, s] = (value[:, :BS] + own_r[i, s].astype(jnp.float32)).astype(jnp.bfloat16)
        g_new_ref[1, i, s] = (value[:, BS:] + own_i[i, s].astype(jnp.float32)).astype(jnp.bfloat16)
        return carry

    lax.fori_loop(0, NB * SLOTS, finish, 0)


def mix_kernel(shifts_ref, pairs_ref, couple_ref, before, here, after, out_ref, line):
    half = WMAX * 2
    line[:half] = before[...].astype(jnp.float32)
    line[half : half + 2 * Z] = here[...].astype(jnp.float32)
    line[half + 2 * Z :] = after[...].astype(jnp.float32)
    for e in range(Z):
        for k in range(2):
            total = jnp.zeros((CHUNK, BS), jnp.float32)
            for q in range(NQ):
                source = pairs_ref[k, q]
                up = (e + WMAX + shifts_ref[q]) * 2 + source
                down = (e + WMAX - shifts_ref[q]) * 2 + source
                total += couple_ref[0, q] * line[up] + couple_ref[1, q] * line[down]
            out_ref[e * 2 + k] = total.astype(jnp.bfloat16)


SMEM = pl.BlockSpec(memory_space=pltpu.SMEM)
VMEM = pl.BlockSpec(memory_space=pltpu.VMEM)


def run_products(tile, cols, blocks, sigma, grad_h):
    return pl.pallas_call(
        products_kernel,
        out_shape=(
            jax.ShapeDtypeStruct((2, NB, SLOTS, ROWS, BS), jnp.bfloat16),
            jax.ShapeDtypeStruct((2, NB, ROWS, BS), jnp.bfloat16),
        ),
        in_specs=[SMEM] * 2 + [VMEM] * 16,
        out_specs=(VMEM, VMEM),
        scratch_shapes=[
            pltpu.VMEM((NB, NB, 2 * BS, 2 * BS), jnp.bfloat16),
            pltpu.VMEM((NB, BS, NB * 2 * BS), jnp.bfloat16),
            pltpu.VMEM((NB, 2 * BS, 2 * BS), jnp.bfloat16),
            pltpu.VMEM((NB, NB * ROWS, 2 * BS), jnp.float32),
        ],
        name="products",
    )(tile, cols, *blocks, sigma, grad_h)


def local(g_zero, sigma_prev, grad_h, cols, shifts, pairs, couple):
    own = g_zero[0, 0]
    tile = lax.axis_index("tile").astype(jnp.int32).reshape(1)
    chunks = [own[0], own[1]]
    right = [along_tile(c, 1, 0, 2) for c in chunks]
    left = [along_tile(c, -1, 1, 3) for c in chunks]
    right2 = [along_tile(c, 1, 1, 2) for c in right]
    left2 = [along_tile(c, -1, 1, 2) for c in left]
    right3 = [along_tile(c, 1, 2, 2) for c in right2]
    left3 = [along_tile(c, -1, 1, 1) for c in left2]
    blocks = chunks + right + left + right2 + left2 + right3 + left3
    g_new, sand = run_products(tile, cols, blocks, sigma_prev[0, 0], grad_h)
    parts = sand.reshape(2 * Z, CHUNK, BS)
    here = lax.all_to_all(parts, ("z", "kpoint"), 0, 0, tiled=True)
    before = along_lines(here[Z:], 1)
    after = along_lines(here[:Z], -1)
    mixed = pl.pallas_call(
        mix_kernel,
        out_shape=jax.ShapeDtypeStruct((2 * Z, CHUNK, BS), jnp.bfloat16),
        in_specs=[SMEM] * 3 + [VMEM] * 3,
        out_specs=VMEM,
        scratch_shapes=[pltpu.VMEM((2 * (Z + 2 * WMAX), CHUNK, BS), jnp.float32)],
        name="mix",
    )(shifts, pairs, couple, before, here, after)
    back = lax.all_to_all(mixed, ("z", "kpoint"), 0, 0, tiled=True)
    return g_new[None, None], back.reshape(1, 1, 2, NB, ROWS, BS)


def solution(mesh):
    devices = mesh.devices.reshape(2, LINES // 2, Z, 2, TILES)
    fine = Mesh(devices, ("yh", "x", "z", "kpoint", "tile"))
    energy = ("yh", "x", "z")
    return jax.shard_map(
        local,
        mesh=fine,
        in_specs=(
            P(energy, "kpoint", None, None, None, "tile", None),
            P(energy, "kpoint", None, None, None, None),
            P(),
            P(),
            P(),
            P(),
            P(),
        ),
        out_specs=(
            P(energy, "kpoint", None, None, None, "tile", None),
            P(energy, "kpoint", None, None, "tile", None),
        ),
        check_vma=False,
    )
```

```python
import jax
import jax.numpy as jnp
from jax import lax
from jax.experimental import pallas as pl
from jax.experimental.pallas import tpu as pltpu
from jax.sharding import Mesh, PartitionSpec as P


BS = 128
NB = 6
SLOTS = 4
NQ = 4
WMAX = 6
TILES = 4
ROWS = BS // TILES
Z = 12
LINES = 8
CHUNK = 16


EDGES = [(0, 1), (1, 0), (2, 3), (3, 2)]
MIDDLE = [(1, 2), (2, 1)]
OUTWARD = [(1, 0), (2, 3)]
HELD = (
    {1: "x1", 2: "x2", 3: "x3"},
    {0: "x1", 2: "y1", 3: "y2"},
    {3: "x1", 1: "y1", 0: "y2"},
    {2: "x1", 1: "x2", 0: "x3"},
)


def gather_tile(chunks):
    def swap(blocks, route):
        return [lax.ppermute(block, "tile", route) for block in blocks]

    x1 = swap(chunks, EDGES)
    y1 = swap(chunks, MIDDLE)
    x2 = swap(y1, OUTWARD)
    y2 = swap(x1, MIDDLE)
    x3 = swap(y2, OUTWARD)
    return chunks + x1 + y1 + x2 + y2 + x3


def to_next_line(block):
    route = []
    for line in range(LINES):
        for z in range(Z):
            target = line + 1 if z >= WMAX else line - 1
            if 0 <= target < LINES:
                route.append((line * Z + z, target * Z + z))
    return lax.ppermute(block, ("yh", "x", "z"), route)


def dot(left, right):
    return jnp.dot(left, right, preferred_element_type=jnp.float32)


def sandwich_kernel(tile_ref, cols_ref, *refs):
    held = {"own": refs[0:2], "x1": refs[2:4], "y1": refs[4:6], "x2": refs[6:8], "y2": refs[8:10], "x3": refs[10:12]}
    sigma_ref, grad_ref, sand_ref, dense, rows_ref, prod, weights, diags, halves = refs[12:]
    tile = tile_ref[0]

    for i in range(NB):
        for c in range(NB):
            if i == c:
                continue
            present = cols_ref[1, i] == c
            for s in range(2, SLOTS):
                present = jnp.logical_or(present, cols_ref[s, i] == c)

            @pl.when(jnp.logical_not(present))
            def _(i=i, c=c):
                dense[c, i] = jnp.zeros((2 * BS, 2 * BS), jnp.bfloat16)

    for m in range(NB):
        re = sigma_ref[0, m]
        im = sigma_ref[1, m]
        weights[m, :BS, :BS] = re
        weights[m, :BS, BS:] = im
        weights[m, BS:, :BS] = -im
        weights[m, BS:, BS:] = re

    for me in range(TILES):

        @pl.when(tile == me)
        def _(me=me):
            def place(b, carry):
                i = b // SLOTS
                s = b % SLOTS
                c = cols_ref[s, i]
                for p in range(TILES):
                    re_ref, im_ref = held["own" if p == me else HELD[me][p]]
                    re = re_ref[i, s]
                    im = im_ref[i, s]
                    top = pl.ds(p * ROWS, ROWS)
                    low = pl.ds(BS + p * ROWS, ROWS)
                    dense[c, i, top, :BS] = re
                    dense[c, i, top, BS:] = im
                    dense[c, i, low, :BS] = -im
                    dense[c, i, low, BS:] = re
                return carry

            lax.fori_loop(0, NB * SLOTS, place, 0)

    for m in range(NB):
        left = dense[m, :, :BS, :].reshape(NB * BS, 2 * BS)
        a = dot(left, weights[m]).astype(jnp.bfloat16)
        prod[:, :, m * 2 * BS : (m + 1) * 2 * BS] = a.reshape(NB, BS, 2 * BS)

    for c in range(NB):
        column = dense[c].reshape(NB * 2 * BS, 2 * BS)
        diag = dot(prod[c], column) + dense[c, c, :BS, :].astype(jnp.float32)
        diag = diag.astype(jnp.bfloat16)
        diags[c, :BS] = diag[:, :BS]
        diags[c, BS:] = diag[:, BS:]
    for c in range(NB):
        g_m = lax.dot_general(
            diags[c], grad_ref[c], (((1,), (1,)), ((), ())), preferred_element_type=jnp.float32
        ).astype(jnp.bfloat16)
        halves[c, :, :BS] = g_m[:BS]
        halves[c, :, BS:] = g_m[BS:]
    mine = pl.ds(pl.multiple_of(tile * ROWS, ROWS), ROWS)
    for c in range(NB):
        sand = dot(grad_ref[c, mine, :], halves[c]).astype(jnp.bfloat16)
        sand_ref[0, c] = sand[:, :BS]
        sand_ref[1, c] = sand[:, BS:]
    rows_ref[...] = prod[:, mine, :].reshape(NB * ROWS, NB * 2 * BS)


def update_kernel(cols_ref, own_r, own_i, dense, rows_ref, g_new_ref, sums):
    rows = rows_ref[...]
    for c in range(NB):
        sums[c] = dot(rows, dense[c].reshape(NB * 2 * BS, 2 * BS))

    for i in range(NB):
        for s in range(SLOTS):
            c = cols_ref[s, i]
            value = sums[c, i * ROWS : (i + 1) * ROWS, :]
            g_new_ref[0, i, s] = (value[:, :BS] + own_r[i, s].astype(jnp.float32)).astype(jnp.bfloat16)
            g_new_ref[1, i, s] = (value[:, BS:] + own_i[i, s].astype(jnp.float32)).astype(jnp.bfloat16)


def mix_kernel(shifts_ref, pairs_ref, couple_ref, parts_ref, out_ref, line):
    for z in range(Z):
        other = z - WMAX if z >= WMAX else WMAX + Z + z
        for k in range(2):
            line[(z + WMAX) * 2 + k] = parts_ref[z * 2 + k, 0].astype(jnp.float32)
            line[other * 2 + k] = parts_ref[z * 2 + k, 1].astype(jnp.float32)
    for e in range(Z):
        for k in range(2):
            total = jnp.zeros((CHUNK, BS), jnp.float32)
            for q in range(NQ):
                source = pairs_ref[k, q]
                up = (e + WMAX + shifts_ref[q]) * 2 + source
                down = (e + WMAX - shifts_ref[q]) * 2 + source
                total += couple_ref[0, q] * line[up] + couple_ref[1, q] * line[down]
            out_ref[e * 2 + k] = total.astype(jnp.bfloat16)


SMEM = pl.BlockSpec(memory_space=pltpu.SMEM)
VMEM = pl.BlockSpec(memory_space=pltpu.VMEM)


MIB = 1 << 20


def run_sandwich(tile, slots, blocks, sigma, grad_h):
    return pl.pallas_call(
        sandwich_kernel,
        out_shape=(
            jax.ShapeDtypeStruct((2, NB, ROWS, BS), jnp.bfloat16),
            jax.ShapeDtypeStruct((NB, NB, 2 * BS, 2 * BS), jnp.bfloat16),
            jax.ShapeDtypeStruct((NB * ROWS, NB * 2 * BS), jnp.bfloat16),
        ),
        in_specs=[SMEM] * 2 + [VMEM] * 14,
        out_specs=(VMEM, VMEM, VMEM),
        scratch_shapes=[
            pltpu.VMEM((NB, BS, NB * 2 * BS), jnp.bfloat16),
            pltpu.VMEM((NB, 2 * BS, 2 * BS), jnp.bfloat16),
            pltpu.VMEM((NB, 2 * BS, BS), jnp.bfloat16),
            pltpu.VMEM((NB, BS, 2 * BS), jnp.bfloat16),
        ],
        compiler_params=pltpu.CompilerParams(vmem_limit_bytes=18 * MIB),
        cost_estimate=pl.CostEstimate(flops=1_500_000_000, bytes_accessed=3_000_000, transcendentals=0),
        name="sandwich",
    )(tile, slots, *blocks, sigma, grad_h)


def run_update(slots, own, dense, rows):
    return pl.pallas_call(
        update_kernel,
        out_shape=jax.ShapeDtypeStruct((2, NB, SLOTS, ROWS, BS), jnp.bfloat16),
        in_specs=[SMEM] + [VMEM] * 4,
        out_specs=VMEM,
        scratch_shapes=[pltpu.VMEM((NB, NB * ROWS, 2 * BS), jnp.float32)],
        compiler_params=pltpu.CompilerParams(vmem_limit_bytes=10 * MIB),
        cost_estimate=pl.CostEstimate(flops=1_000_000_000, bytes_accessed=1_000_000, transcendentals=0),
        name="update",
    )(slots, *own, dense, rows)


def run_mix(shifts, pairs, couple, parts):
    return pl.pallas_call(
        mix_kernel,
        out_shape=jax.ShapeDtypeStruct((2 * Z, CHUNK, BS), jnp.bfloat16),
        in_specs=[SMEM] * 3 + [VMEM],
        out_specs=VMEM,
        scratch_shapes=[pltpu.VMEM((2 * (Z + 2 * WMAX), CHUNK, BS), jnp.float32)],
        compiler_params=pltpu.CompilerParams(vmem_limit_bytes=2 * MIB),
        cost_estimate=pl.CostEstimate(flops=1_000_000, bytes_accessed=400_000, transcendentals=0),
        name="mix",
    )(shifts, pairs, couple, parts)


def local(g_zero, sigma_prev, grad_h, cols, shifts, pairs, couple):
    own = [g_zero[0, 0, 0], g_zero[0, 0, 1]]
    tile = lax.axis_index("tile").astype(jnp.int32).reshape(1)
    slots = cols.T
    sand, dense, rows = run_sandwich(tile, slots, gather_tile(own), sigma_prev[0, 0], grad_h)
    parts = sand.reshape(2 * Z, CHUNK, BS)
    neighbour = to_next_line(parts)
    g_new = run_update(slots, own, dense, rows)
    here = lax.all_to_all(jnp.stack([parts, neighbour], 1), ("z", "kpoint"), 0, 0, tiled=True)
    mixed = run_mix(shifts, pairs, couple, here)
    back = lax.all_to_all(mixed, ("z", "kpoint"), 0, 0, tiled=True)
    return g_new[None, None], back.reshape(1, 1, 2, NB, ROWS, BS)


def solution(mesh):
    devices = mesh.devices.reshape(2, LINES // 2, Z, 2, TILES)
    fine = Mesh(devices, ("yh", "x", "z", "kpoint", "tile"))
    energy = ("yh", "x", "z")
    return jax.shard_map(
        local,
        mesh=fine,
        in_specs=(
            P(energy, "kpoint", None, None, None, "tile", None),
            P(energy, "kpoint", None, None, None, None),
            P(),
            P(),
            P(),
            P(),
            P(),
        ),
        out_specs=(
            P(energy, "kpoint", None, None, None, "tile", None),
            P(energy, "kpoint", None, None, "tile", None),
        ),
        check_vma=False,
    )
```

```python
import jax
import jax.numpy as jnp
from jax import lax
from jax.experimental import pallas as pl
from jax.experimental.pallas import tpu as pltpu
from jax.sharding import Mesh, PartitionSpec as P


BS = 128
NB = 6
SLOTS = 4
NQ = 4
WMAX = 6
TILES = 4
ROWS = BS // TILES
Z = 12
LINES = 8
CHUNK = 16


EDGES = [(0, 1), (1, 0), (2, 3), (3, 2)]
MIDDLE = [(1, 2), (2, 1)]
OUTWARD = [(1, 0), (2, 3)]
def swap(block, route):
    return lax.ppermute(block, "tile", route)


def energy_tile_route(tiles, move_line):
    route = []
    for line in range(LINES):
        for z in range(Z):
            target = line
            if move_line:
                target = line + 1 if z >= WMAX else line - 1
            if 0 <= target < LINES:
                for a, b in tiles:
                    route.append(((line * Z + z) * TILES + a, (target * Z + z) * TILES + b))
    return route


def send(block, tiles, move_line):
    return lax.ppermute(block, ("yh", "x", "z", "tile"), energy_tile_route(tiles, move_line))


def dot(left, right):
    return jnp.dot(left, right, preferred_element_type=jnp.float32)


def clear_absent(scalars, dense):
    for i in range(NB):
        for c in range(NB):
            if i == c:
                continue
            present = scalars[1 + NB + i] == c
            for s in range(2, SLOTS):
                present = jnp.logical_or(present, scalars[1 + s * NB + i] == c)

            @pl.when(jnp.logical_not(present))
            def _(i=i, c=c):
                dense[c, i] = jnp.zeros((2 * BS, 2 * BS), jnp.bfloat16)


def place_blocks(scalars, dense, sources):
    flip = scalars[0] >= TILES // 2

    def place(b, carry):
        i = b // SLOTS
        s = b % SLOTS
        c = scalars[1 + s * NB + i]
        for at, ref in sources:
            p = jnp.where(flip, TILES - 1 - at, at) * ROWS
            re = ref[0, i, s]
            im = ref[1, i, s]
            top = pl.ds(pl.multiple_of(p, ROWS), ROWS)
            low = pl.ds(pl.multiple_of(BS + p, ROWS), ROWS)
            dense[c, i, top, :BS] = re
            dense[c, i, top, BS:] = im
            dense[c, i, low, :BS] = -im
            dense[c, i, low, BS:] = re
        return carry

    lax.fori_loop(0, NB * SLOTS, place, 0)


def make_weights(sigma, weights):
    for m in range(NB):
        re = sigma[0, m]
        im = sigma[1, m]
        weights[m, :BS, :BS] = re
        weights[m, :BS, BS:] = im
        weights[m, BS:, :BS] = -im
        weights[m, BS:, BS:] = re


def prepare_kernel(scalars, own, sigma, grad_in, x1, dense, weights, grad_out):
    clear_absent(scalars, dense)
    place_blocks(scalars, dense, [(0, x1), (1, own)])
    make_weights(sigma, weights)
    grad_out[...] = grad_in[...]


def sandwich_kernel(
    scalars, dense_in, weights, grad, y1, y2, mine_ref, ends_ref, dense, prod, diags, halves
):
    tile = scalars[0]
    place_blocks(scalars, dense, [(2, y1), (3, y2)])

    for m in range(NB):
        left = dense[m, :, :BS, :].reshape(NB * BS, 2 * BS)
        a = dot(left, weights[m]).astype(jnp.bfloat16)
        prod[:, :, m * 2 * BS : (m + 1) * 2 * BS] = a.reshape(NB, BS, 2 * BS)

    for c in range(NB):
        column = dense[c].reshape(NB * 2 * BS, 2 * BS)
        diag = dot(prod[c], column) + dense[c, c, :BS, :].astype(jnp.float32)
        diag = diag.astype(jnp.bfloat16)
        diags[c, :BS] = diag[:, :BS]
        diags[c, BS:] = diag[:, BS:]
    for c in range(NB):
        g_m = lax.dot_general(
            diags[c], grad[c], (((1,), (1,)), ((), ())), preferred_element_type=jnp.float32
        ).astype(jnp.bfloat16)
        halves[c, :, :BS] = g_m[:BS]
        halves[c, :, BS:] = g_m[BS:]
    mine = pl.ds(pl.multiple_of(tile * ROWS, ROWS), ROWS)
    outer = jnp.where(tile < TILES // 2, 0, TILES - 1) * ROWS
    outer = pl.ds(pl.multiple_of(outer, ROWS), ROWS)
    for c in range(NB):
        left = jnp.concatenate([grad[c, mine, :], grad[c, outer, :]], axis=0)
        sand = dot(left, halves[c]).astype(jnp.bfloat16)
        mine_ref[0, c] = sand[:ROWS, :BS]
        mine_ref[1, c] = sand[:ROWS, BS:]
        ends_ref[0, c] = sand[ROWS:, :BS]
        ends_ref[1, c] = sand[ROWS:, BS:]


def update_kernel(
    scalars, own_hbm, sigma_hbm, x1, y1, x2, y2, x3, g_new_ref,
    own, sigma, dense, weights, rows, sums, sems,
):
    copies = [
        pltpu.make_async_copy(own_hbm, own, sems.at[0]),
        pltpu.make_async_copy(sigma_hbm, sigma, sems.at[1]),
    ]
    for copy in copies:
        copy.start()
    tile = scalars[0]
    inner = jnp.logical_or(tile == 1, tile == 2)
    clear_absent(scalars, dense)
    copies[0].wait()

    @pl.when(inner)
    def _():
        place_blocks(scalars, dense, [(0, x1), (1, own), (2, y1), (3, y2)])

    @pl.when(jnp.logical_not(inner))
    def _():
        place_blocks(scalars, dense, [(0, own), (1, x1), (2, x2), (3, x3)])

    copies[1].wait()
    make_weights(sigma, weights)
    mine = pl.ds(pl.multiple_of(tile * ROWS, ROWS), ROWS)
    for m in range(NB):
        left = dense[m, :, mine, :].reshape(NB * ROWS, 2 * BS)
        rows[:, m * 2 * BS : (m + 1) * 2 * BS] = dot(left, weights[m]).astype(jnp.bfloat16)
    for c in range(NB):
        sums[c] = dot(rows[...], dense[c].reshape(NB * 2 * BS, 2 * BS))

    for i in range(NB):
        for s in range(SLOTS):
            c = scalars[1 + s * NB + i]
            value = sums[c, i * ROWS : (i + 1) * ROWS, :]
            for part in range(2):
                old = own[part, i, s].astype(jnp.float32)
                g_new_ref[part, i, s] = (value[:, part * BS : (part + 1) * BS] + old).astype(jnp.bfloat16)


def mix_kernel(shifts_ref, pairs_ref, couple_ref, parts_ref, out_ref, line):
    for z in range(Z):
        other = z - WMAX if z >= WMAX else WMAX + Z + z
        for k in range(2):
            line[(z + WMAX) * 2 + k] = parts_ref[z * 2 + k, 0].astype(jnp.float32)
            line[other * 2 + k] = parts_ref[z * 2 + k, 1].astype(jnp.float32)
    for e in range(Z):
        for k in range(2):
            total = jnp.zeros((CHUNK, BS), jnp.float32)
            for q in range(NQ):
                source = pairs_ref[k, q]
                up = (e + WMAX + shifts_ref[q]) * 2 + source
                down = (e + WMAX - shifts_ref[q]) * 2 + source
                total += couple_ref[0, q] * line[up] + couple_ref[1, q] * line[down]
            out_ref[e * 2 + k] = total.astype(jnp.bfloat16)


SMEM = pl.BlockSpec(memory_space=pltpu.SMEM)
VMEM = pl.BlockSpec(memory_space=pltpu.VMEM)
HBM = pl.BlockSpec(memory_space=pltpu.HBM)


MIB = 1 << 20


BLOCKS = (2, NB, SLOTS, ROWS, BS)
SIGMA = (2, NB, BS, BS)
DENSE = (NB, NB, 2 * BS, 2 * BS)
WEIGHTS = (NB, 2 * BS, 2 * BS)
SAND = jax.ShapeDtypeStruct((2, NB, ROWS, BS), jnp.bfloat16)


def bf16(shape):
    return pltpu.VMEM(shape, jnp.bfloat16)


def run_prepare(scalars, own, sigma, grad_h, x1):
    return pl.pallas_call(
        prepare_kernel,
        out_shape=(
            jax.ShapeDtypeStruct(DENSE, jnp.bfloat16),
            jax.ShapeDtypeStruct(WEIGHTS, jnp.bfloat16),
            jax.ShapeDtypeStruct((NB, BS, BS), jnp.bfloat16),
        ),
        in_specs=[SMEM] + [VMEM] * 4,
        out_specs=(VMEM, VMEM, VMEM),
        compiler_params=pltpu.CompilerParams(vmem_limit_bytes=10 * MIB),
        cost_estimate=pl.CostEstimate(flops=0, bytes_accessed=3_000_000, transcendentals=0),
        name="prepare",
    )(scalars, own, sigma, grad_h, x1)


def run_sandwich(scalars, dense, weights, grad, y1, y2):
    return pl.pallas_call(
        sandwich_kernel,
        out_shape=(SAND, SAND, jax.ShapeDtypeStruct(DENSE, jnp.bfloat16)),
        in_specs=[SMEM] + [VMEM] * 5,
        out_specs=(VMEM, VMEM, VMEM),
        input_output_aliases={1: 2},
        scratch_shapes=[
            bf16((NB, BS, NB * 2 * BS)),
            bf16((NB, 2 * BS, BS)),
            bf16((NB, BS, 2 * BS)),
        ],
        compiler_params=pltpu.CompilerParams(vmem_limit_bytes=18 * MIB),
        cost_estimate=pl.CostEstimate(flops=1_500_000_000, bytes_accessed=3_000_000, transcendentals=0),
        name="sandwich",
    )(scalars, dense, weights, grad, y1, y2)[:2]


def run_update(scalars, own, sigma, x1, y1, x2, y2, x3):
    return pl.pallas_call(
        update_kernel,
        out_shape=jax.ShapeDtypeStruct(BLOCKS, jnp.bfloat16),
        in_specs=[SMEM] + [HBM] * 2 + [VMEM] * 5,
        out_specs=VMEM,
        scratch_shapes=[
            bf16(BLOCKS),
            bf16(SIGMA),
            bf16(DENSE),
            bf16(WEIGHTS),
            bf16((NB * ROWS, NB * 2 * BS)),
            pltpu.VMEM((NB, NB * ROWS, 2 * BS), jnp.float32),
            pltpu.SemaphoreType.DMA((2,)),
        ],
        compiler_params=pltpu.CompilerParams(vmem_limit_bytes=18 * MIB),
        cost_estimate=pl.CostEstimate(flops=1_500_000_000, bytes_accessed=3_000_000, transcendentals=0),
        name="update",
    )(scalars, own, sigma, x1, y1, x2, y2, x3)


def run_mix(shifts, pairs, couple, parts):
    return pl.pallas_call(
        mix_kernel,
        out_shape=jax.ShapeDtypeStruct((2 * Z, CHUNK, BS), jnp.bfloat16),
        in_specs=[SMEM] * 3 + [VMEM],
        out_specs=VMEM,
        scratch_shapes=[pltpu.VMEM((2 * (Z + 2 * WMAX), CHUNK, BS), jnp.float32)],
        compiler_params=pltpu.CompilerParams(vmem_limit_bytes=2 * MIB),
        cost_estimate=pl.CostEstimate(flops=1_000_000, bytes_accessed=400_000, transcendentals=0),
        name="mix",
    )(shifts, pairs, couple, parts)


def local(g_zero, sigma_prev, grad_h, cols, shifts, pairs, couple):
    own = g_zero[0, 0]
    sigma = sigma_prev[0, 0]
    tile = lax.axis_index("tile").astype(jnp.int32)
    inner = jnp.logical_or(tile == 1, tile == 2)
    scalars = jnp.concatenate([tile.reshape(1), cols.T.reshape(-1)])
    x1 = swap(own, EDGES)
    y1 = swap(own, MIDDLE)
    y2 = swap(x1, MIDDLE)
    x2 = swap(y1, OUTWARD)
    dense, weights, grad = run_prepare(scalars, own, sigma, grad_h, x1)
    mine, ends = run_sandwich(scalars, dense, weights, grad, y1, y2)
    mine = mine.reshape(2 * Z, CHUNK, BS)
    ends = ends.reshape(2 * Z, CHUNK, BS)
    outer_own = send(ends, OUTWARD, False)
    inner_next = send(mine, [(1, 1), (2, 2)], True)
    outer_next = send(ends, OUTWARD, True)
    late, inner_next = lax.optimization_barrier((y2, inner_next))
    x3 = swap(late, OUTWARD)
    parts = jnp.stack([jnp.where(inner, mine, outer_own), jnp.where(inner, inner_next, outer_next)], 1)
    here = lax.all_to_all(parts, ("z", "kpoint"), 0, 0, tiled=True)
    mixed = run_mix(shifts, pairs, couple, here)
    back = lax.all_to_all(mixed, ("z", "kpoint"), 0, 0, tiled=True)
    g_new = run_update(scalars, own, sigma, x1, y1, x2, y2, x3)
    return g_new[None, None], back.reshape(1, 1, 2, NB, ROWS, BS)


def solution(mesh):
    devices = mesh.devices.reshape(2, LINES // 2, Z, 2, TILES)
    fine = Mesh(devices, ("yh", "x", "z", "kpoint", "tile"))
    energy = ("yh", "x", "z")
    return jax.shard_map(
        local,
        mesh=fine,
        in_specs=(
            P(energy, "kpoint", None, None, None, "tile", None),
            P(energy, "kpoint", None, None, None, None),
            P(),
            P(),
            P(),
            P(),
            P(),
        ),
        out_specs=(
            P(energy, "kpoint", None, None, None, "tile", None),
            P(energy, "kpoint", None, None, "tile", None),
        ),
        check_vma=False,
    )
```

```python
import jax
import jax.numpy as jnp
from jax import lax
from jax.experimental import pallas as pl
from jax.experimental.pallas import tpu as pltpu
from jax.sharding import Mesh, PartitionSpec as P


BS = 128
NB = 6
SLOTS = 4
NQ = 4
WMAX = 6
TILES = 4
ROWS = BS // TILES
Z = 12
LINES = 8
CHUNK = 16


EDGES = [(0, 1), (1, 0), (2, 3), (3, 2)]
MIDDLE = [(1, 2), (2, 1)]
OUTWARD = [(1, 0), (2, 3)]
ACROSS = [(0, 2), (3, 1)]
def swap(block, route):
    return lax.ppermute(block, "tile", route)


def energy_tile_route(tiles, move_line):
    route = []
    for line in range(LINES):
        for z in range(Z):
            target = line
            if move_line:
                target = line + 1 if z >= WMAX else line - 1
            if 0 <= target < LINES:
                for a, b in tiles:
                    route.append(((line * Z + z) * TILES + a, (target * Z + z) * TILES + b))
    return route


def send(block, tiles, move_line):
    return lax.ppermute(block, ("yh", "x", "z", "tile"), energy_tile_route(tiles, move_line))


def dot(left, right):
    return jnp.dot(left, right, preferred_element_type=jnp.float32)


def clear_absent(scalars, dense):
    for i in range(NB):
        for c in range(NB):
            if i == c:
                continue
            present = scalars[1 + NB + i] == c
            for s in range(2, SLOTS):
                present = jnp.logical_or(present, scalars[1 + s * NB + i] == c)

            @pl.when(jnp.logical_not(present))
            def _(i=i, c=c):
                dense[c, i] = jnp.zeros((2 * BS, 2 * BS), jnp.bfloat16)


def place_blocks(scalars, dense, sources):
    flip = scalars[0] >= TILES // 2

    def place(b, carry):
        i = b // SLOTS
        s = b % SLOTS
        c = scalars[1 + s * NB + i]
        for at, ref in sources:
            p = jnp.where(flip, TILES - 1 - at, at) * ROWS
            re = ref[0, i, s]
            im = ref[1, i, s]
            top = pl.ds(pl.multiple_of(p, ROWS), ROWS)
            low = pl.ds(pl.multiple_of(BS + p, ROWS), ROWS)
            dense[c, i, top, :BS] = re
            dense[c, i, top, BS:] = im
            dense[c, i, low, :BS] = -im
            dense[c, i, low, BS:] = re
        return carry

    lax.fori_loop(0, NB * SLOTS, place, 0)


def make_weights(sigma, weights):
    for m in range(NB):
        re = sigma[0, m]
        im = sigma[1, m]
        weights[m, :BS, :BS] = re
        weights[m, :BS, BS:] = im
        weights[m, BS:, :BS] = -im
        weights[m, BS:, BS:] = re


def prepare_kernel(scalars, own, sigma, grad_in, dense, weights, grad_out):
    clear_absent(scalars, dense)
    place_blocks(scalars, dense, [(1, own)])
    make_weights(sigma, weights)
    grad_out[...] = grad_in[...]


def sandwich_kernel(
    scalars, dense_in, weights, grad, x1, y1, y2, mine_ref, ends_ref, dense, prod, diags, halves
):
    tile = scalars[0]
    place_blocks(scalars, dense, [(0, x1), (2, y1), (3, y2)])

    for m in range(NB):
        left = dense[m, :, :BS, :].reshape(NB * BS, 2 * BS)
        a = dot(left, weights[m]).astype(jnp.bfloat16)
        prod[:, :, m * 2 * BS : (m + 1) * 2 * BS] = a.reshape(NB, BS, 2 * BS)

    for c in range(NB):
        column = dense[c].reshape(NB * 2 * BS, 2 * BS)
        diag = dot(prod[c], column) + dense[c, c, :BS, :].astype(jnp.float32)
        diag = diag.astype(jnp.bfloat16)
        diags[c, :BS] = diag[:, :BS]
        diags[c, BS:] = diag[:, BS:]
    for c in range(NB):
        g_m = lax.dot_general(
            diags[c], grad[c], (((1,), (1,)), ((), ())), preferred_element_type=jnp.float32
        ).astype(jnp.bfloat16)
        halves[c, :, :BS] = g_m[:BS]
        halves[c, :, BS:] = g_m[BS:]
    mine = pl.ds(pl.multiple_of(tile * ROWS, ROWS), ROWS)
    outer = jnp.where(tile < TILES // 2, 0, TILES - 1) * ROWS
    outer = pl.ds(pl.multiple_of(outer, ROWS), ROWS)
    for c in range(NB):
        left = jnp.concatenate([grad[c, mine, :], grad[c, outer, :]], axis=0)
        sand = dot(left, halves[c]).astype(jnp.bfloat16)
        mine_ref[0, c] = sand[:ROWS, :BS]
        mine_ref[1, c] = sand[:ROWS, BS:]
        ends_ref[0, c] = sand[ROWS:, :BS]
        ends_ref[1, c] = sand[ROWS:, BS:]


def update_kernel(
    scalars, own_hbm, sigma_hbm, x1, y1, x2, y2, x3, g_new_ref,
    own, sigma, dense, weights, rows, sums, sems,
):
    copies = [
        pltpu.make_async_copy(own_hbm, own, sems.at[0]),
        pltpu.make_async_copy(sigma_hbm, sigma, sems.at[1]),
    ]
    for copy in copies:
        copy.start()
    tile = scalars[0]
    inner = jnp.logical_or(tile == 1, tile == 2)
    clear_absent(scalars, dense)
    copies[0].wait()

    @pl.when(inner)
    def _():
        place_blocks(scalars, dense, [(0, x1), (1, own), (2, y1), (3, y2)])

    @pl.when(jnp.logical_not(inner))
    def _():
        place_blocks(scalars, dense, [(0, own), (1, x1), (2, x2), (3, x3)])

    copies[1].wait()
    make_weights(sigma, weights)
    mine = pl.ds(pl.multiple_of(tile * ROWS, ROWS), ROWS)
    for m in range(NB):
        left = dense[m, :, mine, :].reshape(NB * ROWS, 2 * BS)
        rows[:, m * 2 * BS : (m + 1) * 2 * BS] = dot(left, weights[m]).astype(jnp.bfloat16)
    for c in range(NB):
        sums[c] = dot(rows[...], dense[c].reshape(NB * 2 * BS, 2 * BS))

    for i in range(NB):
        for s in range(SLOTS):
            c = scalars[1 + s * NB + i]
            value = sums[c, i * ROWS : (i + 1) * ROWS, :]
            for part in range(2):
                old = own[part, i, s].astype(jnp.float32)
                g_new_ref[part, i, s] = (value[:, part * BS : (part + 1) * BS] + old).astype(jnp.bfloat16)


def pack_kernel(scalars, mine, inner_next, outer_own, outer_next, parts):
    tile = scalars[0]
    inner = jnp.logical_or(tile == 1, tile == 2)

    @pl.when(inner)
    def _():
        parts[:, 0] = mine[...]
        parts[:, 1] = inner_next[...]

    @pl.when(jnp.logical_not(inner))
    def _():
        parts[:, 0] = outer_own[...]
        parts[:, 1] = outer_next[...]


def mix_kernel(shifts_ref, pairs_ref, couple_ref, parts_ref, out_ref, line):
    for z in range(Z):
        other = z - WMAX if z >= WMAX else WMAX + Z + z
        for k in range(2):
            line[(z + WMAX) * 2 + k] = parts_ref[z * 2 + k, 0].astype(jnp.float32)
            line[other * 2 + k] = parts_ref[z * 2 + k, 1].astype(jnp.float32)
    for e in range(Z):
        for k in range(2):
            total = jnp.zeros((CHUNK, BS), jnp.float32)
            for q in range(NQ):
                source = pairs_ref[k, q]
                up = (e + WMAX + shifts_ref[q]) * 2 + source
                down = (e + WMAX - shifts_ref[q]) * 2 + source
                total += couple_ref[0, q] * line[up] + couple_ref[1, q] * line[down]
            out_ref[e * 2 + k] = total.astype(jnp.bfloat16)


SMEM = pl.BlockSpec(memory_space=pltpu.SMEM)
VMEM = pl.BlockSpec(memory_space=pltpu.VMEM)
HBM = pl.BlockSpec(memory_space=pltpu.HBM)


MIB = 1 << 20


BLOCKS = (2, NB, SLOTS, ROWS, BS)
SIGMA = (2, NB, BS, BS)
DENSE = (NB, NB, 2 * BS, 2 * BS)
WEIGHTS = (NB, 2 * BS, 2 * BS)
SAND = jax.ShapeDtypeStruct((2, NB, ROWS, BS), jnp.bfloat16)


def bf16(shape):
    return pltpu.VMEM(shape, jnp.bfloat16)


def run_prepare(scalars, own, sigma, grad_h):
    return pl.pallas_call(
        prepare_kernel,
        out_shape=(
            jax.ShapeDtypeStruct(DENSE, jnp.bfloat16),
            jax.ShapeDtypeStruct(WEIGHTS, jnp.bfloat16),
            jax.ShapeDtypeStruct((NB, BS, BS), jnp.bfloat16),
        ),
        in_specs=[SMEM] + [VMEM] * 3,
        out_specs=(VMEM, VMEM, VMEM),
        compiler_params=pltpu.CompilerParams(vmem_limit_bytes=10 * MIB),
        cost_estimate=pl.CostEstimate(flops=0, bytes_accessed=3_000_000, transcendentals=0),
        name="prepare",
    )(scalars, own, sigma, grad_h)


def run_sandwich(scalars, dense, weights, grad, x1, y1, y2):
    return pl.pallas_call(
        sandwich_kernel,
        out_shape=(SAND, SAND, jax.ShapeDtypeStruct(DENSE, jnp.bfloat16)),
        in_specs=[SMEM] + [VMEM] * 6,
        out_specs=(VMEM, VMEM, VMEM),
        input_output_aliases={1: 2},
        scratch_shapes=[
            bf16((NB, BS, NB * 2 * BS)),
            bf16((NB, 2 * BS, BS)),
            bf16((NB, BS, 2 * BS)),
        ],
        compiler_params=pltpu.CompilerParams(vmem_limit_bytes=18 * MIB),
        cost_estimate=pl.CostEstimate(flops=1_500_000_000, bytes_accessed=3_000_000, transcendentals=0),
        name="sandwich",
    )(scalars, dense, weights, grad, x1, y1, y2)[:2]


def run_update(scalars, own, sigma, x1, y1, x2, y2, x3):
    return pl.pallas_call(
        update_kernel,
        out_shape=jax.ShapeDtypeStruct(BLOCKS, jnp.bfloat16),
        in_specs=[SMEM] + [HBM] * 2 + [VMEM] * 5,
        out_specs=VMEM,
        scratch_shapes=[
            bf16(BLOCKS),
            bf16(SIGMA),
            bf16(DENSE),
            bf16(WEIGHTS),
            bf16((NB * ROWS, NB * 2 * BS)),
            pltpu.VMEM((NB, NB * ROWS, 2 * BS), jnp.float32),
            pltpu.SemaphoreType.DMA((2,)),
        ],
        compiler_params=pltpu.CompilerParams(vmem_limit_bytes=18 * MIB),
        cost_estimate=pl.CostEstimate(flops=1_500_000_000, bytes_accessed=3_000_000, transcendentals=0),
        name="update",
    )(scalars, own, sigma, x1, y1, x2, y2, x3)


def run_pack(scalars, mine, inner_next, outer_own, outer_next):
    return pl.pallas_call(
        pack_kernel,
        out_shape=jax.ShapeDtypeStruct((2 * Z, 2, CHUNK, BS), jnp.bfloat16),
        in_specs=[SMEM] + [VMEM] * 4,
        out_specs=VMEM,
        compiler_params=pltpu.CompilerParams(vmem_limit_bytes=2 * MIB),
        cost_estimate=pl.CostEstimate(flops=0, bytes_accessed=400_000, transcendentals=0),
        name="pack",
    )(scalars, mine, inner_next, outer_own, outer_next)


def run_mix(shifts, pairs, couple, parts):
    return pl.pallas_call(
        mix_kernel,
        out_shape=jax.ShapeDtypeStruct((2 * Z, CHUNK, BS), jnp.bfloat16),
        in_specs=[SMEM] * 3 + [VMEM],
        out_specs=VMEM,
        scratch_shapes=[pltpu.VMEM((2 * (Z + 2 * WMAX), CHUNK, BS), jnp.float32)],
        compiler_params=pltpu.CompilerParams(vmem_limit_bytes=2 * MIB),
        cost_estimate=pl.CostEstimate(flops=1_000_000, bytes_accessed=400_000, transcendentals=0),
        name="mix",
    )(shifts, pairs, couple, parts)


def local(g_zero, sigma_prev, grad_h, cols, shifts, pairs, couple):
    own = g_zero[0, 0]
    sigma = sigma_prev[0, 0]
    tile = lax.axis_index("tile").astype(jnp.int32)
    scalars = jnp.concatenate([tile.reshape(1), cols.T.reshape(-1)])
    y2 = swap(own, ACROSS)
    y1 = swap(own, MIDDLE)
    x1 = swap(own, EDGES)
    x2 = swap(y1, OUTWARD)
    dense, weights, grad = run_prepare(scalars, own, sigma, grad_h)
    mine, ends = run_sandwich(scalars, dense, weights, grad, x1, y1, y2)
    mine = mine.reshape(2 * Z, CHUNK, BS)
    ends = ends.reshape(2 * Z, CHUNK, BS)
    inner_next = send(mine, [(1, 1), (2, 2)], True)
    outer_next = send(ends, OUTWARD, True)
    outer_own = send(ends, OUTWARD, False)
    late, inner_next = lax.optimization_barrier((y2, inner_next))
    x3 = swap(late, OUTWARD)
    parts = run_pack(scalars, mine, inner_next, outer_own, outer_next)
    here = lax.all_to_all(parts, ("z", "kpoint"), 0, 0, tiled=True)
    mixed = run_mix(shifts, pairs, couple, here)
    back = lax.all_to_all(mixed, ("z", "kpoint"), 0, 0, tiled=True)
    g_new = run_update(scalars, own, sigma, x1, y1, x2, y2, x3)
    return g_new[None, None], back.reshape(1, 1, 2, NB, ROWS, BS)


def solution(mesh):
    devices = mesh.devices.reshape(2, LINES // 2, Z, 2, TILES)
    fine = Mesh(devices, ("yh", "x", "z", "kpoint", "tile"))
    energy = ("yh", "x", "z")
    return jax.shard_map(
        local,
        mesh=fine,
        in_specs=(
            P(energy, "kpoint", None, None, None, "tile", None),
            P(energy, "kpoint", None, None, None, None),
            P(),
            P(),
            P(),
            P(),
            P(),
        ),
        out_specs=(
            P(energy, "kpoint", None, None, None, "tile", None),
            P(energy, "kpoint", None, None, "tile", None),
        ),
        check_vma=False,
    )
```
